32 devices in a mesh: nodes: 8 (over y, x, core), cols: 4 (over z).
Axes of the slice: x: 2, y: 2, z: 4, core: 2. Of those that a mesh axis runs over, the one named last changes fastest.
Arguments:
- features: bfloat16 [1024, 512], P('nodes', 'cols'), may hold values from -6 to 6
- weight: bfloat16 [512, 512], P(None, 'cols'), may hold values from -0.25 to 0.25
- degree: int32 [1024], P('nodes'), may hold values from 1 to 64
- tile_cols: int32 [8, 8], P('nodes'), may hold values from 0 to 7, as said below
- tile_count: int32 [8], P('nodes'), may hold values from 1 to 8, as said below
- tile_codes: int32 [8, 8], P('nodes'), may hold values from 0 to 1048575
- cotangent: bfloat16 [1024, 512], P('nodes', 'cols'), may hold values from -6 to 6
Outputs:
- activation: bfloat16 [1024, 512], P('nodes', 'cols')
- weight_grad: float32 [512, 512], P(None, 'cols')
- feats_grad: float32 [1024, 512], P('nodes', 'cols')
The draws below stay inside these ranges and needn't reach their ends.
Inputs may be any that keep to these rules, and one draw needn't show every extreme that they name: `tile_cols`: each row lists every node block once, and row i begins with block i. The tiles of row block i are those of its first tile_count[i] slots; some row block holds all 8.
All inputs are finite; a program needn't handle non-finite values.
Results may differ from the reference program's by a relative error of at most 0.0065.
Values may be sent and summed in bfloat16 or wider, within the bound.
A program may use at most 64 MiB of HBM per device.

```python
import jax
import jax.numpy as jnp
from jax import lax

H = 512
TILE = 128
BLOCKS = 8
NODES = 1024


def draw_tile_cols(key, part):
    keys = jax.random.split(key, BLOCKS)
    shuffled = jax.vmap(lambda one_key: jax.random.permutation(one_key, BLOCKS - 1))(keys).astype(jnp.int32)
    offsets = jnp.concatenate([jnp.zeros((BLOCKS, 1), jnp.int32), shuffled + 1], axis=1)
    row_ids = jnp.arange(BLOCKS, dtype=jnp.int32)[:, None]
    return ((row_ids + offsets) % BLOCKS).astype(jnp.int32)


def draw_tile_count(key, part):
    first_key, second_key = jax.random.split(key)
    drawn = jax.random.randint(first_key, (BLOCKS,), 1, BLOCKS + 1, dtype=jnp.int32)
    counts = jnp.maximum(drawn * (drawn + BLOCKS) // (2 * BLOCKS), 1)
    fullest = jax.random.randint(second_key, (), 0, BLOCKS, dtype=jnp.int32)
    return jnp.where(jnp.arange(BLOCKS, dtype=jnp.int32) == fullest, BLOCKS, counts).astype(jnp.int32)


def set_ends(values, own_key, least, high):
    shape = values.shape
    place = [jax.random.randint(jax.random.fold_in(own_key, axis), (), 0, shape[axis]) for axis in range(len(shape))]
    values = values.at[tuple(place)].set(least)
    longest = shape.index(max(shape))
    place[longest] = (place[longest] + 1) % shape[longest]
    return values.at[tuple(place)].set(high)


def steps_of(key, dims, shards, smallest, high):
    loudness, own = 1.0, jax.random.fold_in(key, 6)
    for axis_at, blocks in shards:
        heights = jnp.exp(jax.random.uniform(jax.random.fold_in(own, axis_at), (blocks,), jnp.float32, smallest / len(shards), high / len(shards)))
        loudness = loudness * jnp.repeat(heights, dims[axis_at] // blocks).reshape([-1 if axis == axis_at else 1 for axis in range(len(dims))])
    return loudness


def centred(own_key, dims, deviation, most, cuts=(), kind=jnp.bfloat16):
    values = jax.random.normal(own_key, dims, jnp.float32) * deviation
    if len(cuts) > 0:
        values = steps_of(own_key, dims, cuts, -0.22, 0.18) * values
    return jnp.clip(values, min=-most, max=most).astype(kind)


def setup_inputs(seed: int = 0) -> dict:
    splits = jax.random.split(jax.random.key(seed), 8)
    return {
        "features": centred(splits[0], (NODES, H), 1.0, 6.0, ((0, 8), (1, 4))),
        "weight": centred(splits[1], (H, H), H ** -0.5, 0.25, ((1, 4),)),
        "degree": set_ends(jax.random.randint(splits[2], (NODES,), 1, 65), jax.random.fold_in(splits[2], 1), 1, 64).astype(jnp.int32),
        "tile_cols": draw_tile_cols(jax.random.fold_in(splits[7], 71), 0),
        "tile_count": draw_tile_count(jax.random.fold_in(splits[7], 71), 0),
        "tile_codes": set_ends(jax.random.randint(splits[5], (BLOCKS, BLOCKS), 0, 1048576), jax.random.fold_in(splits[5], 1), 0, 1048575).astype(jnp.int32),
        "cotangent": centred(splits[6], (NODES, H), 1.0, 6.0, ((0, 8), (1, 4))),
    }


def tile_bits(pattern_code):
    line_ids = jnp.arange(TILE, dtype=jnp.int32)
    hashed = pattern_code[..., None, None] * 73856093 ^ line_ids[:, None] * 19349663 ^ line_ids[None, :] * 83492791
    hashed = hashed ^ hashed >> 13
    hashed = hashed * 1274126177
    hashed = hashed ^ hashed >> 16
    return hashed & 63 == 0

def make_tiles(matches, code_table, live_limit, own, identity):
    slot_ids = jnp.arange(matches.shape[1], dtype=jnp.int32)
    slot_index = lax.optimization_barrier(jnp.sum(jnp.where(matches, slot_ids[None, :], 0), axis=1, dtype=jnp.int32))
    code_value = lax.optimization_barrier(jnp.sum(jnp.where(matches, code_table, 0), axis=1, dtype=jnp.int32))
    pattern = tile_bits(code_value) & (slot_index < live_limit)[:, None, None]
    values = pattern.astype(jnp.float32) + jnp.where(own, 1.0, 0.0).astype(jnp.float32)[:, None, None] * identity
    return values.astype(jnp.bfloat16)

def reference(features, weight, degree, tile_cols, tile_count, tile_codes, cotangent):
    blocks = tile_cols.shape[0]
    block_ids = jnp.arange(blocks, dtype=jnp.int32)
    identity = jnp.eye(TILE, dtype=jnp.float32)
    inv_root = lax.rsqrt(degree.astype(jnp.float32))[:, None]
    scaled = (features.astype(jnp.float32) * inv_root).astype(jnp.bfloat16)
    scaled_wide = lax.optimization_barrier(scaled).astype(jnp.float32)

    def adjacency_rows(row):
        matches = tile_cols[row][None, :] == block_ids[:, None]
        tiles = make_tiles(matches, tile_codes[row][None, :], tile_count[row], block_ids == row, identity)
        return jnp.transpose(tiles.astype(jnp.float32), (1, 0, 2)).reshape(TILE, blocks * TILE)

    def forward_rows(row):
        return jnp.dot(adjacency_rows(row), scaled_wide, preferred_element_type=jnp.float32)
    gathered = lax.map(forward_rows, block_ids).reshape(blocks * TILE, H)
    aggregated = (inv_root * gathered).astype(jnp.bfloat16)
    pre = jnp.dot(aggregated, weight, preferred_element_type=jnp.float32)
    activation = jax.nn.silu(pre).astype(jnp.bfloat16)
    sigma = jax.nn.sigmoid(pre)
    grad_pre = (cotangent.astype(jnp.float32) * sigma * (1.0 + pre * (1.0 - sigma))).astype(jnp.bfloat16)
    weight_grad = lax.dot_general(aggregated, grad_pre, (((0,), (0,)), ((), ())), preferred_element_type=jnp.float32)
    grad_agg = lax.dot_general(grad_pre, weight, (((1,), (1,)), ((), ())), preferred_element_type=jnp.float32)
    grad_scaled = (inv_root * grad_agg).astype(jnp.bfloat16)
    grad_wide = lax.optimization_barrier(grad_scaled).astype(jnp.float32)

    def backward_rows(total, row):
        block_grad = lax.dynamic_slice_in_dim(grad_wide, row * TILE, TILE, 0)
        term = lax.dot_general(adjacency_rows(row), block_grad, (((0,), (0,)), ((), ())), preferred_element_type=jnp.float32)
        return (total + term, None)
    back_total, _ = lax.scan(backward_rows, jnp.zeros((blocks * TILE, H), jnp.float32), block_ids)
    feats_grad = inv_root * back_total
    return (activation, weight_grad, feats_grad)
```

```python
import functools

import jax
import jax.numpy as jnp
from jax import lax
from jax.experimental import pallas as pl
from jax.experimental.pallas import tpu as pltpu
from jax.sharding import PartitionSpec as P

MESH = pl.DeviceIdType.MESH

TILE = 128


def tile_bits(pattern_code):
    line_ids = jnp.arange(TILE, dtype=jnp.int32)
    hashed = (
        pattern_code[..., None, None] * 73856093
        ^ line_ids[:, None] * 19349663
        ^ line_ids[None, :] * 83492791
    )
    hashed = hashed ^ hashed >> 13
    hashed = hashed * 1274126177
    hashed = hashed ^ hashed >> 16
    return hashed & 63 == 0


def make_tiles(matches, code_table, live_limit, own, identity):
    slot_ids = jnp.arange(matches.shape[1], dtype=jnp.int32)
    slot_index = jnp.sum(jnp.where(matches, slot_ids[None, :], 0), axis=1, dtype=jnp.int32)
    code_value = jnp.sum(jnp.where(matches, code_table, 0), axis=1, dtype=jnp.int32)
    pattern = tile_bits(code_value) & (slot_index < live_limit)[:, None, None]
    values = (
        pattern.astype(jnp.float32)
        + jnp.where(own, 1.0, 0.0).astype(jnp.float32)[:, None, None] * identity
    )
    return values.astype(jnp.bfloat16)


def body(features, weight, degree, tile_cols, tile_count, tile_codes, cotangent):
    my_block = lax.axis_index("nodes")
    identity = jnp.eye(TILE, dtype=jnp.float32)
    inv_root = lax.rsqrt(degree.astype(jnp.float32))[:, None]
    scaled = (features.astype(jnp.float32) * inv_root).astype(jnp.bfloat16)
    my_cols = tile_cols[0]
    my_codes = tile_codes[0]
    my_count = tile_count[0]
    pieces = lax.all_gather(scaled[None], "nodes", axis=0, tiled=True)
    count_blocks = pieces.shape[0]
    targets = jnp.arange(count_blocks, dtype=jnp.int32)
    matches = targets[:, None] == my_cols[None, :]
    tiles = make_tiles(matches, my_codes[None, :], my_count, targets == my_block, identity)
    gathered = lax.dot_general(
        tiles, pieces, (((0, 2), (0, 1)), ((), ())), preferred_element_type=jnp.float32
    )
    aggregated = (inv_root * gathered).astype(jnp.bfloat16)
    agg_full = lax.all_gather(aggregated, "cols", axis=1, tiled=True)
    pre = jnp.dot(agg_full, weight, preferred_element_type=jnp.float32)
    activation = jax.nn.silu(pre).astype(jnp.bfloat16)
    sigma = jax.nn.sigmoid(pre)
    grad_pre = (cotangent.astype(jnp.float32) * sigma * (1.0 + pre * (1.0 - sigma))).astype(
        jnp.bfloat16
    )
    partial_grad = lax.dot_general(
        agg_full, grad_pre, (((0,), (0,)), ((), ())), preferred_element_type=jnp.float32
    )
    weight_grad = lax.psum(partial_grad, "nodes")
    terms = lax.dot_general(
        grad_pre, weight, (((1,), (1,)), ((), ())), preferred_element_type=jnp.float32
    )
    grad_agg = lax.psum_scatter(terms, "cols", scatter_dimension=1, tiled=True)
    grad_scaled = (inv_root * grad_agg).astype(jnp.bfloat16)
    all_cols, all_counts, all_codes = (
        lax.all_gather(tile_cols, "nodes", axis=0, tiled=True),
        lax.all_gather(tile_count, "nodes", axis=0, tiled=True),
        lax.all_gather(tile_codes, "nodes", axis=0, tiled=True),
    )
    pieces = lax.all_gather(grad_scaled[None], "nodes", axis=0, tiled=True)
    count_blocks = pieces.shape[0]
    row_ids = jnp.arange(count_blocks, dtype=jnp.int32)
    tiles = make_tiles(all_cols == my_block, all_codes, all_counts, row_ids == my_block, identity)
    back_total = lax.dot_general(
        tiles, pieces, (((0, 1), (0, 1)), ((), ())), preferred_element_type=jnp.float32
    )
    feats_grad = inv_root * back_total
    return (activation, weight_grad, feats_grad)


FUSED_NODES = 8


def dot(a, b, dims):
    return lax.dot_general(a, b, (dims, ((), ())), preferred_element_type=jnp.float32)


def hash_tile(code, base, own, identity):
    shape = base.shape
    hashed = (code * 73856093)[None] ^ base.reshape(shape[0] // 8, 8, shape[1])
    hashed = hashed ^ hashed >> 13
    hashed = hashed * 1274126177
    hashed = hashed ^ hashed >> 16
    bits = jnp.where((hashed & 63 == 0) & (code >= 0)[None], 1.0, 0.0).reshape(shape)
    return (bits + jnp.where(own, 1.0, 0.0) * identity).astype(jnp.bfloat16)


def fused_kernel(
    nodes, cols,
    features, weight, degree, tile_cols, tile_count, tile_codes, cotangent,
    activation, weight_grad, feats_grad,
    feat_all, agg_all, gp_all, gs_all, w_all, tab_out, tab_in, fwd_tiles, bwd_tiles,
    wg_part, wg_in, wg_all,
    feat_send, feat_recv, tab_send, tab_recv, w_send, w_recv, agg_send, agg_recv,
    gp_send, gp_recv, gs_send, gs_recv, rs_send, rs_recv, ag_send, ag_recv,
):
    n = lax.axis_index("nodes")
    c = lax.axis_index("cols")
    node_peers = [(lax.rem(n + d, nodes), c) for d in range(1, nodes)]
    col_peers = [(n, lax.rem(c + d, cols)) for d in range(1, cols)]

    barrier = pltpu.get_barrier_semaphore()
    for peer in node_peers + col_peers:
        pl.semaphore_signal(barrier, inc=1, device_id=peer, device_id_type=MESH)

    def push(src, dst, peer, send, recv):
        copy = pltpu.make_async_remote_copy(
            src_ref=src, dst_ref=dst, send_sem=send, recv_sem=recv, device_id=peer, device_id_type=MESH
        )
        copy.start()
        return copy

    def gather(buffer, me, peers, send, recv):
        return [
            push(buffer.at[me], buffer.at[me], peer, send.at[i], recv.at[i]) for i, peer in enumerate(peers)
        ]

    row_ids = lax.broadcasted_iota(jnp.int32, (TILE, TILE), 0)
    lane_ids = lax.broadcasted_iota(jnp.int32, (TILE, TILE), 1)
    identity = jnp.where(row_ids == lane_ids, 1.0, 0.0)
    inv_row = lax.rsqrt(degree[...].astype(jnp.float32))
    inv_root = jnp.sum(identity * inv_row, axis=1, keepdims=True)
    feat_all[n] = (features[...].astype(jnp.float32) * inv_root).astype(jnp.bfloat16)

    codes = []
    for block in range(nodes):
        code = jnp.int32(-1)
        for slot in range(nodes):
            hit = (tile_cols[0, slot] == block) & (slot < tile_count[0])
            code = jnp.where(hit, tile_codes[0, slot], code)
        codes.append(jnp.full((8, TILE), code, jnp.int32))
        tab_out[block] = codes[-1]

    pl.semaphore_wait(barrier, nodes + cols - 2)

    feat_copies = gather(feat_all, n, node_peers, feat_send, feat_recv)
    tab_copies = [
        push(tab_out.at[peer[0]], tab_in.at[n], peer, tab_send.at[i], tab_recv.at[i])
        for i, peer in enumerate(node_peers)
    ]
    w_copies = [
        push(
            weight.at[pl.ds(pl.multiple_of(peer[1] * TILE, TILE), TILE), :],
            w_all.at[c], peer, w_send.at[i], w_recv.at[i],
        )
        for i, peer in enumerate(col_peers)
    ]
    w_all[c] = weight[pl.ds(pl.multiple_of(c * TILE, TILE), TILE), :]
    tab_in[n] = tab_out[n]

    base = row_ids * 19349663 ^ lane_ids * 83492791
    for block in range(nodes):
        fwd_tiles[:, block * TILE:(block + 1) * TILE] = hash_tile(codes[block], base, n == block, identity)

    for copy in feat_copies:
        copy.wait_recv()
    gathered = dot(fwd_tiles[...], feat_all[...].reshape(nodes * TILE, TILE), ((1,), (0,)))
    agg_all[c] = (inv_root * gathered).astype(jnp.bfloat16)
    agg_copies = gather(agg_all, c, col_peers, agg_send, agg_recv)

    for copy in tab_copies:
        copy.wait_recv()
    base_t = lane_ids * 19349663 ^ row_ids * 83492791
    for block in range(nodes):
        bwd_tiles[:, block * TILE:(block + 1) * TILE] = hash_tile(tab_in[block], base_t, n == block, identity)

    for copy in agg_copies:
        copy.wait_recv()
    pre = dot(agg_all[0], weight[:TILE, :], ((1,), (0,)))
    for q in range(1, cols):
        pre += dot(agg_all[q], weight[q * TILE:(q + 1) * TILE, :], ((1,), (0,)))
    sigma = jax.nn.sigmoid(pre)
    grad_pre = (cotangent[...].astype(jnp.float32) * sigma * (1.0 + pre * (1.0 - sigma))).astype(jnp.bfloat16)
    gp_all[c] = grad_pre
    gp_copies = gather(gp_all, c, col_peers, gp_send, gp_recv)

    rows = wg_part.shape[1]
    for q in range(cols):
        part = dot(agg_all[q], grad_pre, ((0,), (0,)))
        for i in range(TILE // rows):
            wg_part[q * (TILE // rows) + i] = part[i * rows:(i + 1) * rows, :]
    rs_copies = [
        push(wg_part.at[peer[0]], wg_in.at[n], peer, rs_send.at[i], rs_recv.at[i])
        for i, peer in enumerate(node_peers)
    ]
    wg_in[n] = wg_part[n]
    activation[...] = (pre * sigma).astype(jnp.bfloat16)

    for copy in w_copies + gp_copies:
        copy.wait_recv()
    grad_agg = dot(gp_all[0], w_all[0], ((1,), (1,)))
    for q in range(1, cols):
        grad_agg += dot(gp_all[q], w_all[q], ((1,), (1,)))
    gs_all[n] = (inv_root * grad_agg).astype(jnp.bfloat16)
    gs_copies = gather(gs_all, n, node_peers, gs_send, gs_recv)

    for copy in rs_copies:
        copy.wait_recv()
    wg_all[n] = jnp.sum(wg_in[...], axis=0).astype(wg_all.dtype)
    ag_copies = gather(wg_all, n, node_peers, ag_send, ag_recv)

    for copy in gs_copies:
        copy.wait_recv()
    back = dot(bwd_tiles[...], gs_all[...].reshape(nodes * TILE, TILE), ((1,), (0,)))
    feats_grad[...] = inv_root * back

    for copy in ag_copies:
        copy.wait_recv()
    for block in range(nodes):
        weight_grad[block * rows:(block + 1) * rows, :] = wg_all[block].astype(jnp.float32)
    for copy in feat_copies + tab_copies + w_copies + agg_copies + gp_copies + rs_copies + gs_copies + ag_copies:
        copy.wait_send()


def fused(nodes, cols, features, weight, degree, tile_cols, tile_count, tile_codes, cotangent):
    rows = weight.shape[0] // nodes
    vmem = pl.BlockSpec(memory_space=pltpu.VMEM)
    smem = pl.BlockSpec(memory_space=pltpu.SMEM)
    block = (TILE, TILE)
    sems = [pltpu.SemaphoreType.DMA((count - 1,)) for count in (nodes, nodes, cols, cols, cols, nodes, nodes, nodes) for _ in "sr"]
    return pl.pallas_call(
        functools.partial(fused_kernel, nodes, cols),
        out_shape=(
            jax.ShapeDtypeStruct(features.shape, jnp.bfloat16),
            jax.ShapeDtypeStruct(weight.shape, jnp.float32),
            jax.ShapeDtypeStruct(features.shape, jnp.float32),
        ),
        in_specs=[vmem, vmem, vmem, smem, smem, smem, vmem],
        out_specs=(vmem, vmem, vmem),
        scratch_shapes=[
            pltpu.VMEM((nodes,) + block, jnp.bfloat16),
            pltpu.VMEM((cols,) + block, jnp.bfloat16),
            pltpu.VMEM((cols,) + block, jnp.bfloat16),
            pltpu.VMEM((nodes,) + block, jnp.bfloat16),
            pltpu.VMEM((cols,) + block, jnp.bfloat16),
            pltpu.VMEM((nodes, 8, TILE), jnp.int32),
            pltpu.VMEM((nodes, 8, TILE), jnp.int32),
            pltpu.VMEM((TILE, nodes * TILE), jnp.bfloat16),
            pltpu.VMEM((TILE, nodes * TILE), jnp.bfloat16),
            pltpu.VMEM((nodes, rows, TILE), jnp.float32),
            pltpu.VMEM((nodes, rows, TILE), jnp.float32),
            pltpu.VMEM((nodes, rows, TILE), jnp.bfloat16),
        ] + sems,
        compiler_params=pltpu.CompilerParams(collective_id=0, has_side_effects=True),
    )(features, weight, degree[None, :], tile_cols, tile_count, tile_codes, cotangent)


def solution(mesh):
    in_specs = (
        P("nodes", "cols"),
        P(None, "cols"),
        P("nodes"),
        P("nodes", None),
        P("nodes"),
        P("nodes", None),
        P("nodes", "cols"),
    )
    out_specs = (P("nodes", "cols"), P(None, "cols"), P("nodes", "cols"))
    local = body
    if mesh.shape["nodes"] <= FUSED_NODES:
        local = functools.partial(fused, mesh.shape["nodes"], mesh.shape["cols"])
    return jax.shard_map(local, mesh=mesh, in_specs=in_specs, out_specs=out_specs, check_vma=False)
```

```python
import functools

import jax
import jax.numpy as jnp
from jax import lax
from jax.experimental import pallas as pl
from jax.experimental.pallas import tpu as pltpu
from jax.sharding import PartitionSpec as P

MESH = pl.DeviceIdType.MESH

TILE = 128


def tile_bits(pattern_code):
    line_ids = jnp.arange(TILE, dtype=jnp.int32)
    hashed = (
        pattern_code[..., None, None] * 73856093
        ^ line_ids[:, None] * 19349663
        ^ line_ids[None, :] * 83492791
    )
    hashed = hashed ^ hashed >> 13
    hashed = hashed * 1274126177
    hashed = hashed ^ hashed >> 16
    return hashed & 63 == 0


def make_tiles(matches, code_table, live_limit, own, identity):
    slot_ids = jnp.arange(matches.shape[1], dtype=jnp.int32)
    slot_index = jnp.sum(jnp.where(matches, slot_ids[None, :], 0), axis=1, dtype=jnp.int32)
    code_value = jnp.sum(jnp.where(matches, code_table, 0), axis=1, dtype=jnp.int32)
    pattern = tile_bits(code_value) & (slot_index < live_limit)[:, None, None]
    values = (
        pattern.astype(jnp.float32)
        + jnp.where(own, 1.0, 0.0).astype(jnp.float32)[:, None, None] * identity
    )
    return values.astype(jnp.bfloat16)


def body(features, weight, degree, tile_cols, tile_count, tile_codes, cotangent):
    my_block = lax.axis_index("nodes")
    identity = jnp.eye(TILE, dtype=jnp.float32)
    inv_root = lax.rsqrt(degree.astype(jnp.float32))[:, None]
    scaled = (features.astype(jnp.float32) * inv_root).astype(jnp.bfloat16)
    my_cols = tile_cols[0]
    my_codes = tile_codes[0]
    my_count = tile_count[0]
    pieces = lax.all_gather(scaled[None], "nodes", axis=0, tiled=True)
    count_blocks = pieces.shape[0]
    targets = jnp.arange(count_blocks, dtype=jnp.int32)
    matches = targets[:, None] == my_cols[None, :]
    tiles = make_tiles(matches, my_codes[None, :], my_count, targets == my_block, identity)
    gathered = lax.dot_general(
        tiles, pieces, (((0, 2), (0, 1)), ((), ())), preferred_element_type=jnp.float32
    )
    aggregated = (inv_root * gathered).astype(jnp.bfloat16)
    agg_full = lax.all_gather(aggregated, "cols", axis=1, tiled=True)
    pre = jnp.dot(agg_full, weight, preferred_element_type=jnp.float32)
    activation = jax.nn.silu(pre).astype(jnp.bfloat16)
    sigma = jax.nn.sigmoid(pre)
    grad_pre = (cotangent.astype(jnp.float32) * sigma * (1.0 + pre * (1.0 - sigma))).astype(
        jnp.bfloat16
    )
    partial_grad = lax.dot_general(
        agg_full, grad_pre, (((0,), (0,)), ((), ())), preferred_element_type=jnp.float32
    )
    weight_grad = lax.psum(partial_grad, "nodes")
    terms = lax.dot_general(
        grad_pre, weight, (((1,), (1,)), ((), ())), preferred_element_type=jnp.float32
    )
    grad_agg = lax.psum_scatter(terms, "cols", scatter_dimension=1, tiled=True)
    grad_scaled = (inv_root * grad_agg).astype(jnp.bfloat16)
    all_cols, all_counts, all_codes = (
        lax.all_gather(tile_cols, "nodes", axis=0, tiled=True),
        lax.all_gather(tile_count, "nodes", axis=0, tiled=True),
        lax.all_gather(tile_codes, "nodes", axis=0, tiled=True),
    )
    pieces = lax.all_gather(grad_scaled[None], "nodes", axis=0, tiled=True)
    count_blocks = pieces.shape[0]
    row_ids = jnp.arange(count_blocks, dtype=jnp.int32)
    tiles = make_tiles(all_cols == my_block, all_codes, all_counts, row_ids == my_block, identity)
    back_total = lax.dot_general(
        tiles, pieces, (((0, 1), (0, 1)), ((), ())), preferred_element_type=jnp.float32
    )
    feats_grad = inv_root * back_total
    return (activation, weight_grad, feats_grad)


FUSED_NODES = 8


def dot(a, b, dims):
    return lax.dot_general(a, b, (dims, ((), ())), preferred_element_type=jnp.float32)


def hash_tile(code, base, own, identity):
    hashed = (code * 73856093) ^ base
    hashed = hashed ^ hashed >> 13
    hashed = hashed * 1274126177
    hashed = hashed ^ hashed >> 16
    bits = jnp.where((hashed & 63 == 0) & (code >= 0), 1.0, 0.0)
    return (bits + jnp.where(own, 1.0, 0.0) * identity).astype(jnp.bfloat16)


def fused_kernel(
    nodes, cols,
    features_hbm, weight_hbm, degree_hbm, tile_cols_hbm, tile_count_hbm, tile_codes_hbm, cotangent_hbm,
    activation, weight_grad, feats_grad,
    features, weight, degree, tile_cols, tile_count, tile_codes, cotangent,
    feat_all, agg_all, gp_all, gs_all, w_all, tab_out, tab_in, fwd_tiles, bwd_tiles,
    wg_part, wg_pair, wg_half, wg_in, wg_all,
    load_sem, feat_send, feat_recv, tab_send, tab_recv, w_send, w_recv, agg_send, agg_recv,
    gp_send, gp_recv, gs_send, gs_recv, pair_send, pair_recv, rs_send, rs_recv, ag_send, ag_recv,
):
    n = lax.axis_index("nodes")
    c = lax.axis_index("cols")
    chips = nodes // 2
    chip, core = n // 2, lax.rem(n, 2)
    partner = n + 1 - 2 * core
    node_peers = [(lax.rem(n + d, nodes), c) for d in range(1, nodes)]
    col_peers = [(n, lax.rem(c + d, cols)) for d in range(1, cols)]
    twins = [lax.rem(n + 2 * d, nodes) for d in range(1, chips)]
    senders = [lax.rem(n + nodes - 2 * d, nodes) for d in range(1, chips)]

    barrier = pltpu.get_barrier_semaphore()
    for peer in node_peers + col_peers:
        pl.semaphore_signal(barrier, inc=1, device_id=peer, device_id_type=MESH)

    loads = []
    for i, (src, dst) in enumerate((
        (degree_hbm, degree), (features_hbm, features), (tile_cols_hbm, tile_cols), (tile_count_hbm, tile_count),
        (tile_codes_hbm, tile_codes), (weight_hbm, weight), (cotangent_hbm, cotangent),
    )):
        loads.append(pltpu.make_async_copy(src, dst, load_sem.at[i]))
        loads[-1].start()

    sent = []

    def push(src, dst, peer, send, recv):
        copy = pltpu.make_async_remote_copy(
            src_ref=src, dst_ref=dst, send_sem=send, recv_sem=recv, device_id=peer, device_id_type=MESH
        )
        copy.start()
        sent.append(copy)
        return copy

    def push_block(buffer, slot, peer, i, send, recv):
        return push(buffer.at[slot], buffer.at[slot], peer, send.at[i], recv.at[i])

    def spread(buffer, send, recv):
        far = [push_block(buffer, n, (twin, c), i, send, recv) for i, twin in enumerate(twins)]
        return far, [push_block(buffer, n, (partner, c), chips - 1, send, recv)]

    def pass_on(buffer, far, near, send, recv):
        for i, sender in enumerate(senders):
            far[i].wait_recv()
            near.append(push_block(buffer, sender, (partner, c), chips + i, send, recv))

    def gather_cols(buffer, send, recv):
        return [push_block(buffer, c, peer, i, send, recv) for i, peer in enumerate(col_peers)]

    row_ids = lax.broadcasted_iota(jnp.int32, (TILE, TILE), 0)
    lane_ids = lax.broadcasted_iota(jnp.int32, (TILE, TILE), 1)
    identity = jnp.where(row_ids == lane_ids, 1.0, 0.0)
    base = row_ids * 19349663 ^ lane_ids * 83492791
    loads[0].wait()
    inv_row = lax.rsqrt(degree[...].astype(jnp.float32))
    inv_root = jnp.sum(identity * inv_row, axis=1, keepdims=True)
    loads[1].wait()
    feat_all[n] = (features[...].astype(jnp.float32) * inv_root).astype(jnp.bfloat16)

    for load in loads[2:5]:
        load.wait()
    for block in range(nodes):
        code = jnp.int32(-1)
        for slot in range(nodes):
            hit = (tile_cols[0, slot] == block) & (slot < tile_count[0])
            code = jnp.where(hit, tile_codes[0, slot], code)
        tab_out[block] = jnp.full((1, TILE), code, jnp.int32)
    loads[5].wait()

    pl.semaphore_wait(barrier, nodes + cols - 2)

    feat_far, feat_near = spread(feat_all, feat_send, feat_recv)
    tab_copies = [
        push(tab_out.at[peer[0]], tab_in.at[n], peer, tab_send.at[i], tab_recv.at[i])
        for i, peer in enumerate(node_peers)
    ]
    w_copies = [
        push(
            weight.at[pl.ds(pl.multiple_of(peer[1] * TILE, TILE), TILE), :],
            w_all.at[c], peer, w_send.at[i], w_recv.at[i],
        )
        for i, peer in enumerate(col_peers)
    ]
    w_all[c] = weight[pl.ds(pl.multiple_of(c * TILE, TILE), TILE), :]
    tab_in[n] = tab_out[n]

    for block in range(nodes):
        fwd_tiles[:, block * TILE:(block + 1) * TILE] = hash_tile(tab_out[block], base, n == block, identity)

    pass_on(feat_all, feat_far, feat_near, feat_send, feat_recv)
    for copy in feat_near:
        copy.wait_recv()
    gathered = dot(fwd_tiles[...], feat_all[...].reshape(nodes * TILE, TILE), ((1,), (0,)))
    agg_all[c] = (inv_root * gathered).astype(jnp.bfloat16)
    agg_copies = gather_cols(agg_all, agg_send, agg_recv)

    for copy in tab_copies:
        copy.wait_recv()
    base_t = lane_ids * 19349663 ^ row_ids * 83492791
    for block in range(nodes):
        bwd_tiles[:, block * TILE:(block + 1) * TILE] = hash_tile(tab_in[block], base_t, n == block, identity)
    loads[6].wait()

    for copy in agg_copies:
        copy.wait_recv()
    pre = dot(agg_all[0], weight[:TILE, :], ((1,), (0,)))
    for q in range(1, cols):
        pre += dot(agg_all[q], weight[q * TILE:(q + 1) * TILE, :], ((1,), (0,)))
    sigma = jax.nn.sigmoid(pre)
    grad_pre = (cotangent[...].astype(jnp.float32) * sigma * (1.0 + pre * (1.0 - sigma))).astype(jnp.bfloat16)
    gp_all[c] = grad_pre
    gp_copies = gather_cols(gp_all, gp_send, gp_recv)

    rows = wg_in.shape[1]
    for q in range(cols):
        part = dot(agg_all[q], grad_pre, ((0,), (0,)))
        for i in range(TILE // rows):
            owner = q * (TILE // rows) + i
            wg_part[owner % 2, owner // 2] = part[i * rows:(i + 1) * rows, :]
    pair = push(wg_part.at[1 - core], wg_pair, (partner, c), pair_send, pair_recv)
    activation[...] = (pre * sigma).astype(jnp.bfloat16)
    pair.wait_recv()
    wg_half[...] = wg_part[core] + wg_pair[...]
    rs_copies = [
        push(wg_half.at[twin // 2], wg_in.at[i], (twin, c), rs_send.at[i], rs_recv.at[i])
        for i, twin in enumerate(twins)
    ]

    for copy in w_copies + gp_copies:
        copy.wait_recv()
    grad_agg = dot(gp_all[0], w_all[0], ((1,), (1,)))
    for q in range(1, cols):
        grad_agg += dot(gp_all[q], w_all[q], ((1,), (1,)))
    gs_all[n] = (inv_root * grad_agg).astype(jnp.bfloat16)
    gs_far, gs_near = spread(gs_all, gs_send, gs_recv)

    for copy in rs_copies:
        copy.wait_recv()
    wg_all[n] = (wg_half[chip] + jnp.sum(wg_in[...], axis=0)).astype(wg_all.dtype)
    ag_far, ag_near = spread(wg_all, ag_send, ag_recv)

    pass_on(gs_all, gs_far, gs_near, gs_send, gs_recv)
    pass_on(wg_all, ag_far, ag_near, ag_send, ag_recv)
    for copy in gs_near:
        copy.wait_recv()
    back = dot(bwd_tiles[...], gs_all[...].reshape(nodes * TILE, TILE), ((1,), (0,)))
    feats_grad[...] = inv_root * back

    for copy in ag_near:
        copy.wait_recv()
    for block in range(nodes):
        weight_grad[block * rows:(block + 1) * rows, :] = wg_all[block].astype(jnp.float32)
    for copy in sent:
        copy.wait_send()


def write_out_kernel(*refs):
    count = len(refs) // 2
    copies = [pltpu.make_async_copy(refs[i], refs[count + i], refs[-1].at[i]) for i in range(count)]
    for copy in copies:
        copy.start()
    for copy in copies:
        copy.wait()


def fused(nodes, cols, features, weight, degree, tile_cols, tile_count, tile_codes, cotangent):
    rows = weight.shape[0] // nodes
    chips = nodes // 2
    anywhere = pl.BlockSpec(memory_space=pl.ANY)
    vmem = pl.BlockSpec(memory_space=pltpu.VMEM)
    block = (TILE, TILE)
    outs = ((features.shape, jnp.bfloat16), (weight.shape, jnp.float32), (features.shape, jnp.float32))
    hops = 2 * chips - 1
    dma = pltpu.SemaphoreType.DMA
    results = pl.pallas_call(
        functools.partial(fused_kernel, nodes, cols),
        out_shape=tuple(pltpu.VMEM(shape, dtype) for shape, dtype in outs),
        in_specs=[anywhere] * 7,
        out_specs=(vmem, vmem, vmem),
        scratch_shapes=[
            pltpu.VMEM(features.shape, jnp.bfloat16),
            pltpu.VMEM(weight.shape, jnp.bfloat16),
            pltpu.VMEM((1, TILE), jnp.int32),
            pltpu.SMEM(tile_cols.shape, jnp.int32),
            pltpu.SMEM(tile_count.shape, jnp.int32),
            pltpu.SMEM(tile_codes.shape, jnp.int32),
            pltpu.VMEM(cotangent.shape, jnp.bfloat16),
            pltpu.VMEM((nodes,) + block, jnp.bfloat16),
            pltpu.VMEM((cols,) + block, jnp.bfloat16),
            pltpu.VMEM((cols,) + block, jnp.bfloat16),
            pltpu.VMEM((nodes,) + block, jnp.bfloat16),
            pltpu.VMEM((cols,) + block, jnp.bfloat16),
            pltpu.VMEM((nodes, 1, TILE), jnp.int32),
            pltpu.VMEM((nodes, 1, TILE), jnp.int32),
            pltpu.VMEM((TILE, nodes * TILE), jnp.bfloat16),
            pltpu.VMEM((TILE, nodes * TILE), jnp.bfloat16),
            pltpu.VMEM((2, chips, rows, TILE), jnp.float32),
            pltpu.VMEM((chips, rows, TILE), jnp.float32),
            pltpu.VMEM((chips, rows, TILE), jnp.float32),
            pltpu.VMEM((chips - 1, rows, TILE), jnp.float32),
            pltpu.VMEM((nodes, rows, TILE), jnp.bfloat16),
            dma((7,)),
            dma((hops,)), dma((hops,)),
            dma((nodes - 1,)), dma((nodes - 1,)),
            dma((cols - 1,)), dma((cols - 1,)),
            dma((cols - 1,)), dma((cols - 1,)),
            dma((cols - 1,)), dma((cols - 1,)),
            dma((hops,)), dma((hops,)),
            dma, dma,
            dma((chips - 1,)), dma((chips - 1,)),
            dma((hops,)), dma((hops,)),
        ],
        compiler_params=pltpu.CompilerParams(collective_id=0, has_side_effects=True),
        name="layer",
    )(features, weight, degree[None, :], tile_cols, tile_count, tile_codes, cotangent)
    return pl.pallas_call(
        write_out_kernel,
        out_shape=tuple(jax.ShapeDtypeStruct(shape, dtype) for shape, dtype in outs),
        in_specs=[vmem] * 3,
        out_specs=(anywhere,) * 3,
        scratch_shapes=[dma((3,))],
        name="write_out",
    )(*[pltpu.with_memory_space_constraint(x, pltpu.VMEM) for x in results])


def solution(mesh):
    in_specs = (
        P("nodes", "cols"),
        P(None, "cols"),
        P("nodes"),
        P("nodes", None),
        P("nodes"),
        P("nodes", None),
        P("nodes", "cols"),
    )
    out_specs = (P("nodes", "cols"), P(None, "cols"), P("nodes", "cols"))
    local = body
    if mesh.shape["nodes"] <= FUSED_NODES:
        local = functools.partial(fused, mesh.shape["nodes"], mesh.shape["cols"])
    return jax.shard_map(local, mesh=mesh, in_specs=in_specs, out_specs=out_specs, check_vma=False)
```

```python
import functools

import jax
import jax.numpy as jnp
from jax import lax
from jax.experimental import pallas as pl
from jax.experimental.pallas import tpu as pltpu
from jax.sharding import PartitionSpec as P

MESH = pl.DeviceIdType.MESH

TILE = 128


def tile_bits(pattern_code):
    line_ids = jnp.arange(TILE, dtype=jnp.int32)
    hashed = (
        pattern_code[..., None, None] * 73856093
        ^ line_ids[:, None] * 19349663
        ^ line_ids[None, :] * 83492791
    )
    hashed = hashed ^ hashed >> 13
    hashed = hashed * 1274126177
    hashed = hashed ^ hashed >> 16
    return hashed & 63 == 0


def make_tiles(matches, code_table, live_limit, own, identity):
    slot_ids = jnp.arange(matches.shape[1], dtype=jnp.int32)
    slot_index = jnp.sum(jnp.where(matches, slot_ids[None, :], 0), axis=1, dtype=jnp.int32)
    code_value = jnp.sum(jnp.where(matches, code_table, 0), axis=1, dtype=jnp.int32)
    pattern = tile_bits(code_value) & (slot_index < live_limit)[:, None, None]
    values = (
        pattern.astype(jnp.float32)
        + jnp.where(own, 1.0, 0.0).astype(jnp.float32)[:, None, None] * identity
    )
    return values.astype(jnp.bfloat16)


def body(features, weight, degree, tile_cols, tile_count, tile_codes, cotangent):
    my_block = lax.axis_index("nodes")
    identity = jnp.eye(TILE, dtype=jnp.float32)
    inv_root = lax.rsqrt(degree.astype(jnp.float32))[:, None]
    scaled = (features.astype(jnp.float32) * inv_root).astype(jnp.bfloat16)
    my_cols = tile_cols[0]
    my_codes = tile_codes[0]
    my_count = tile_count[0]
    pieces = lax.all_gather(scaled[None], "nodes", axis=0, tiled=True)
    count_blocks = pieces.shape[0]
    targets = jnp.arange(count_blocks, dtype=jnp.int32)
    matches = targets[:, None] == my_cols[None, :]
    tiles = make_tiles(matches, my_codes[None, :], my_count, targets == my_block, identity)
    gathered = lax.dot_general(
        tiles, pieces, (((0, 2), (0, 1)), ((), ())), preferred_element_type=jnp.float32
    )
    aggregated = (inv_root * gathered).astype(jnp.bfloat16)
    agg_full = lax.all_gather(aggregated, "cols", axis=1, tiled=True)
    pre = jnp.dot(agg_full, weight, preferred_element_type=jnp.float32)
    activation = jax.nn.silu(pre).astype(jnp.bfloat16)
    sigma = jax.nn.sigmoid(pre)
    grad_pre = (cotangent.astype(jnp.float32) * sigma * (1.0 + pre * (1.0 - sigma))).astype(
        jnp.bfloat16
    )
    partial_grad = lax.dot_general(
        agg_full, grad_pre, (((0,), (0,)), ((), ())), preferred_element_type=jnp.float32
    )
    weight_grad = lax.psum(partial_grad, "nodes")
    terms = lax.dot_general(
        grad_pre, weight, (((1,), (1,)), ((), ())), preferred_element_type=jnp.float32
    )
    grad_agg = lax.psum_scatter(terms, "cols", scatter_dimension=1, tiled=True)
    grad_scaled = (inv_root * grad_agg).astype(jnp.bfloat16)
    all_cols, all_counts, all_codes = (
        lax.all_gather(tile_cols, "nodes", axis=0, tiled=True),
        lax.all_gather(tile_count, "nodes", axis=0, tiled=True),
        lax.all_gather(tile_codes, "nodes", axis=0, tiled=True),
    )
    pieces = lax.all_gather(grad_scaled[None], "nodes", axis=0, tiled=True)
    count_blocks = pieces.shape[0]
    row_ids = jnp.arange(count_blocks, dtype=jnp.int32)
    tiles = make_tiles(all_cols == my_block, all_codes, all_counts, row_ids == my_block, identity)
    back_total = lax.dot_general(
        tiles, pieces, (((0, 1), (0, 1)), ((), ())), preferred_element_type=jnp.float32
    )
    feats_grad = inv_root * back_total
    return (activation, weight_grad, feats_grad)


FUSED_NODES = 8


def dot(a, b, dims):
    return lax.dot_general(a, b, (dims, ((), ())), preferred_element_type=jnp.float32)


def hash_tile(code, base, own, identity):
    hashed = (code * 73856093) ^ base
    hashed = hashed ^ hashed >> 13
    hashed = hashed * 1274126177
    hashed = hashed ^ hashed >> 16
    bits = jnp.where((hashed & 63 == 0) & (code >= 0), 1.0, 0.0)
    return (bits + jnp.where(own, 1.0, 0.0) * identity).astype(jnp.bfloat16)


def fused_kernel(
    nodes, cols,
    features_hbm, weight_hbm, degree_hbm, tile_cols_hbm, tile_count_hbm, tile_codes_hbm, cotangent_hbm,
    activation, weight_grad, feats_grad,
    features, weight, degree, tile_cols, tile_count, tile_codes, cotangent,
    feat_all, agg_all, gp_all, gs_all, w_all, tab_out, tab_in, fwd_tiles, bwd_tiles,
    wg_part, wg_pair, wg_half, wg_in, wg_all,
    load_sem, feat_send, feat_recv, tab_send, tab_recv, w_send, w_recv, agg_send, agg_recv,
    gp_send, gp_recv, gs_send, gs_recv, pair_send, pair_recv, rs_send, rs_recv, ag_send, ag_recv,
):
    n = lax.axis_index("nodes")
    c = lax.axis_index("cols")
    chips = nodes // 2
    chip, core = n // 2, lax.rem(n, 2)
    partner = n + 1 - 2 * core
    node_peers = [(lax.rem(n + d, nodes), c) for d in range(1, nodes)]
    col_peers = [(n, lax.rem(c + d, cols)) for d in range(1, cols)]
    twins = [lax.rem(n + 2 * d, nodes) for d in range(1, chips)]
    senders = [lax.rem(n + nodes - 2 * d, nodes) for d in range(1, chips)]

    barrier = pltpu.get_barrier_semaphore()
    for peer in node_peers + col_peers:
        pl.semaphore_signal(barrier, inc=1, device_id=peer, device_id_type=MESH)

    loads = []
    for i, (src, dst) in enumerate((
        (degree_hbm, degree), (features_hbm, features), (tile_cols_hbm, tile_cols), (tile_count_hbm, tile_count),
        (tile_codes_hbm, tile_codes), (weight_hbm, weight), (cotangent_hbm, cotangent),
    )):
        loads.append(pltpu.make_async_copy(src, dst, load_sem.at[i]))
        loads[-1].start()

    sent = []

    def push(src, dst, peer, send, recv):
        copy = pltpu.make_async_remote_copy(
            src_ref=src, dst_ref=dst, send_sem=send, recv_sem=recv, device_id=peer, device_id_type=MESH
        )
        copy.start()
        sent.append(copy)
        return copy

    def push_block(buffer, slot, peer, i, send, recv):
        return push(buffer.at[slot], buffer.at[slot], peer, send.at[i], recv.at[i])

    def spread(buffer, send, recv):
        far = [push_block(buffer, n, (twin, c), i, send, recv) for i, twin in enumerate(twins)]
        return far, [push_block(buffer, n, (partner, c), chips - 1, send, recv)]

    def pass_on(buffer, far, near, send, recv):
        for i, sender in enumerate(senders):
            far[i].wait_recv()
            near.append(push_block(buffer, sender, (partner, c), chips + i, send, recv))

    def gather_cols(buffer, send, recv):
        return [push_block(buffer, c, peer, i, send, recv) for i, peer in enumerate(col_peers)]

    row_ids = lax.broadcasted_iota(jnp.int32, (TILE, TILE), 0)
    lane_ids = lax.broadcasted_iota(jnp.int32, (TILE, TILE), 1)
    identity = jnp.where(row_ids == lane_ids, 1.0, 0.0)
    base = row_ids * 19349663 ^ lane_ids * 83492791
    loads[0].wait()
    inv_row = lax.rsqrt(degree[...].astype(jnp.float32))
    inv_root = jnp.sum(identity * inv_row, axis=1, keepdims=True)
    loads[1].wait()
    feat_all[n] = (features[...].astype(jnp.float32) * inv_root).astype(jnp.bfloat16)

    for load in loads[2:5]:
        load.wait()
    for block in range(nodes):
        code = jnp.int32(-1)
        for slot in range(nodes):
            hit = (tile_cols[0, slot] == block) & (slot < tile_count[0])
            code = jnp.where(hit, tile_codes[0, slot], code)
        tab_out[block] = jnp.full((1, TILE), code, jnp.int32)
    loads[5].wait()

    pl.semaphore_wait(barrier, nodes + cols - 2)

    feat_far, feat_near = spread(feat_all, feat_send, feat_recv)
    tab_copies = [
        push(tab_out.at[peer[0]], tab_in.at[n], peer, tab_send.at[i], tab_recv.at[i])
        for i, peer in enumerate(node_peers)
    ]
    w_copies = [
        push(
            weight.at[pl.ds(pl.multiple_of(peer[1] * TILE, TILE), TILE), :],
            w_all.at[c], peer, w_send.at[i], w_recv.at[i],
        )
        for i, peer in enumerate(col_peers)
    ]
    w_all[c] = weight[pl.ds(pl.multiple_of(c * TILE, TILE), TILE), :]
    tab_in[n] = tab_out[n]

    for block in range(nodes):
        fwd_tiles[:, block * TILE:(block + 1) * TILE] = hash_tile(tab_out[block], base, n == block, identity)

    pass_on(feat_all, feat_far, feat_near, feat_send, feat_recv)
    for copy in feat_near:
        copy.wait_recv()
    gathered = dot(fwd_tiles[...], feat_all[...].reshape(nodes * TILE, TILE), ((1,), (0,)))
    agg_all[c] = (inv_root * gathered).astype(jnp.bfloat16)
    agg_copies = gather_cols(agg_all, agg_send, agg_recv)

    for copy in tab_copies:
        copy.wait_recv()
    base_t = lane_ids * 19349663 ^ row_ids * 83492791
    for block in range(nodes):
        bwd_tiles[:, block * TILE:(block + 1) * TILE] = hash_tile(tab_in[block], base_t, n == block, identity)
    loads[6].wait()

    for copy in agg_copies:
        copy.wait_recv()
    pre = dot(agg_all[0], weight[:TILE, :], ((1,), (0,)))
    for q in range(1, cols):
        pre += dot(agg_all[q], weight[q * TILE:(q + 1) * TILE, :], ((1,), (0,)))
    sigma = jax.nn.sigmoid(pre)
    grad_pre = (cotangent[...].astype(jnp.float32) * sigma * (1.0 + pre * (1.0 - sigma))).astype(jnp.bfloat16)
    gp_all[c] = grad_pre
    gp_copies = gather_cols(gp_all, gp_send, gp_recv)

    rows = wg_in.shape[1]
    for q in range(cols):
        part = dot(agg_all[q], grad_pre, ((0,), (0,)))
        for i in range(TILE // rows):
            owner = q * (TILE // rows) + i
            wg_part[owner % 2, owner // 2] = part[i * rows:(i + 1) * rows, :]
    pair = push(wg_part.at[1 - core], wg_pair, (partner, c), pair_send, pair_recv)
    activation[...] = (pre * sigma).astype(jnp.bfloat16)
    pair.wait_recv()
    wg_half[...] = wg_part[core] + wg_pair[...]
    rs_copies = [
        push(wg_half.at[twin // 2], wg_in.at[i], (twin, c), rs_send.at[i], rs_recv.at[i])
        for i, twin in enumerate(twins)
    ]

    for copy in w_copies + gp_copies:
        copy.wait_recv()
    grad_agg = dot(gp_all[0], w_all[0], ((1,), (1,)))
    for q in range(1, cols):
        grad_agg += dot(gp_all[q], w_all[q], ((1,), (1,)))
    gs_all[n] = (inv_root * grad_agg).astype(jnp.bfloat16)
    gs_far, gs_near = spread(gs_all, gs_send, gs_recv)

    for copy in rs_copies:
        copy.wait_recv()
    wg_all[n] = (wg_half[chip] + jnp.sum(wg_in[...], axis=0)).astype(wg_all.dtype)
    ag_near = [push_block(wg_all, n, peer, i, ag_send, ag_recv) for i, peer in enumerate(node_peers)]

    pass_on(gs_all, gs_far, gs_near, gs_send, gs_recv)
    for copy in gs_near:
        copy.wait_recv()
    back = dot(bwd_tiles[...], gs_all[...].reshape(nodes * TILE, TILE), ((1,), (0,)))
    feats_grad[...] = inv_root * back

    for copy in ag_near:
        copy.wait_recv()
    for block in range(nodes):
        weight_grad[block * rows:(block + 1) * rows, :] = wg_all[block].astype(jnp.float32)
    for copy in sent:
        copy.wait_send()


def write_out_kernel(*refs):
    count = len(refs) // 2
    copies = [pltpu.make_async_copy(refs[i], refs[count + i], refs[-1].at[i]) for i in range(count)]
    for copy in copies:
        copy.start()
    for copy in copies:
        copy.wait()


def fused(nodes, cols, features, weight, degree, tile_cols, tile_count, tile_codes, cotangent):
    rows = weight.shape[0] // nodes
    chips = nodes // 2
    anywhere = pl.BlockSpec(memory_space=pl.ANY)
    vmem = pl.BlockSpec(memory_space=pltpu.VMEM)
    block = (TILE, TILE)
    outs = ((features.shape, jnp.bfloat16), (weight.shape, jnp.float32), (features.shape, jnp.float32))
    hops = 2 * chips - 1
    dma = pltpu.SemaphoreType.DMA
    results = pl.pallas_call(
        functools.partial(fused_kernel, nodes, cols),
        out_shape=tuple(pltpu.VMEM(shape, dtype) for shape, dtype in outs),
        in_specs=[anywhere] * 7,
        out_specs=(vmem, vmem, vmem),
        scratch_shapes=[
            pltpu.VMEM(features.shape, jnp.bfloat16),
            pltpu.VMEM(weight.shape, jnp.bfloat16),
            pltpu.VMEM((1, TILE), jnp.int32),
            pltpu.SMEM(tile_cols.shape, jnp.int32),
            pltpu.SMEM(tile_count.shape, jnp.int32),
            pltpu.SMEM(tile_codes.shape, jnp.int32),
            pltpu.VMEM(cotangent.shape, jnp.bfloat16),
            pltpu.VMEM((nodes,) + block, jnp.bfloat16),
            pltpu.VMEM((cols,) + block, jnp.bfloat16),
            pltpu.VMEM((cols,) + block, jnp.bfloat16),
            pltpu.VMEM((nodes,) + block, jnp.bfloat16),
            pltpu.VMEM((cols,) + block, jnp.bfloat16),
            pltpu.VMEM((nodes, 1, TILE), jnp.int32),
            pltpu.VMEM((nodes, 1, TILE), jnp.int32),
            pltpu.VMEM((TILE, nodes * TILE), jnp.bfloat16),
            pltpu.VMEM((TILE, nodes * TILE), jnp.bfloat16),
            pltpu.VMEM((2, chips, rows, TILE), jnp.float32),
            pltpu.VMEM((chips, rows, TILE), jnp.float32),
            pltpu.VMEM((chips, rows, TILE), jnp.float32),
            pltpu.VMEM((chips - 1, rows, TILE), jnp.float32),
            pltpu.VMEM((nodes, rows, TILE), jnp.bfloat16),
            dma((7,)),
            dma((hops,)), dma((hops,)),
            dma((nodes - 1,)), dma((nodes - 1,)),
            dma((cols - 1,)), dma((cols - 1,)),
            dma((cols - 1,)), dma((cols - 1,)),
            dma((cols - 1,)), dma((cols - 1,)),
            dma((hops,)), dma((hops,)),
            dma, dma,
            dma((chips - 1,)), dma((chips - 1,)),
            dma((hops,)), dma((hops,)),
        ],
        compiler_params=pltpu.CompilerParams(collective_id=0, has_side_effects=True),
        name="layer",
    )(features, weight, degree[None, :], tile_cols, tile_count, tile_codes, cotangent)
    return pl.pallas_call(
        write_out_kernel,
        out_shape=tuple(jax.ShapeDtypeStruct(shape, dtype) for shape, dtype in outs),
        in_specs=[vmem] * 3,
        out_specs=(anywhere,) * 3,
        scratch_shapes=[dma((3,))],
        name="write_out",
    )(*[pltpu.with_memory_space_constraint(x, pltpu.VMEM) for x in results])


def solution(mesh):
    in_specs = (
        P("nodes", "cols"),
        P(None, "cols"),
        P("nodes"),
        P("nodes", None),
        P("nodes"),
        P("nodes", None),
        P("nodes", "cols"),
    )
    out_specs = (P("nodes", "cols"), P(None, "cols"), P("nodes", "cols"))
    local = body
    if mesh.shape["nodes"] <= FUSED_NODES:
        local = functools.partial(fused, mesh.shape["nodes"], mesh.shape["cols"])
    return jax.shard_map(local, mesh=mesh, in_specs=in_specs, out_specs=out_specs, check_vma=False)
```
